32 devices in a mesh: wide: 8 (over z, y), narrow: 4 (over x, core).
Axes of the slice: x: 2, y: 2, z: 4, core: 2. Of those that a mesh axis runs over, the one named last changes fastest.
Arguments:
- solution: float32 [8, 16384], P(None, ('wide', 'narrow')), may hold values from -6 to 6
- residual: float32 [8, 16384], P(None, ('wide', 'narrow')), may hold values from -600 to 600
- direction: float32 [8, 16384], P(None, ('wide', 'narrow')), may hold values from -600 to 600
- error_var: float32 [16384], P(('wide', 'narrow')), may hold values from 0.25 to 2
- footprint: bfloat16 [16384, 4, 128], P(('wide', 'narrow')), may hold values from -0.25 to 0.25
- tiles: int32 [16384, 4], P(('wide', 'narrow')), may hold values from 0 to 1279
- window: int32 [16384, 1], P(('wide', 'narrow')), may hold values from 0 to 7; in each aligned block of 512 rows (0 to 511, 512 to 1023, ...) at most 160 rows name the same one
- temporal: bfloat16 [320, 320], replicated, may hold values from -40 to 40, as said below
- spatial_lat: bfloat16 [128, 128], replicated, may hold values from -40 to 40, as said below
- spatial_lon: bfloat16 [128, 128], replicated, may hold values from -40 to 40, as said below
Outputs:
- solution_new: float32 [8, 16384], P(None, ('wide', 'narrow'))
- residual_new: float32 [8, 16384], P(None, ('wide', 'narrow'))
- direction_new: float32 [8, 16384], P(None, ('wide', 'narrow'))
The draws below stay inside these ranges and needn't reach their ends.
Inputs may be any that keep to these rules, and one draw needn't show every extreme that they name: At most 160 of the observations held by one device share a window, and some device reaches that in every draw. `temporal`: A symmetric positive definite covariance. `spatial_lat`: A symmetric positive definite covariance. `spatial_lon`: A symmetric positive definite covariance.
All inputs are finite; a program needn't handle non-finite values.
Results may differ from the reference program's by a relative error of at most 0.004.
Values may be sent and summed in bfloat16 or wider, within the bound.
A program may use at most 128 MiB of HBM per device.

```python
import math
import jax
import jax.numpy as jnp
import numpy as np
from jax import lax

LAT = 128
LON = 128
DAYS = 320
RHS = 8
NT = 4
OBS_DEV = 512
OBS = 16384
CAP = 160
DAY_DEV = 40
LATB = 32
TILES = 1280
N_WIDE = 8
N_NARROW = 4


def covariance(key, order):
    length = max(order // 2, 1)
    normals = jnp.clip(jax.random.normal(key, (order, order), jnp.float32), -6.0, 6.0)
    position = jnp.arange(order, dtype=jnp.float32)
    decay = jnp.exp(-jnp.abs(position[:, None] - position[None, :]) / length)
    factor = normals * decay
    return jnp.dot(factor, factor.T, precision=lax.Precision.HIGHEST) / order + 0.5 * jnp.eye(order, dtype=jnp.float32)


def state_draw(key, salt):
    key = jax.random.fold_in(key, salt)
    key_rows = jax.random.fold_in(key, 0)
    key_cols = jax.random.fold_in(key, 1)
    key_base = jax.random.fold_in(key, 3)
    position = jnp.arange(OBS, dtype=jnp.float32) / max(OBS - 1, 1)
    row_scale = jnp.exp(jax.random.uniform(key_rows, (OBS,), jnp.float32, 0.0, math.log(10.0))) / math.sqrt(10.0)
    col_scale = jnp.exp(jax.random.uniform(key_cols, (RHS,), jnp.float32, 0.0, math.log(10.0))) / math.sqrt(10.0)
    base = jnp.clip(jax.random.normal(key_base, (RHS, OBS), jnp.float32), -6.0, 6.0)
    trend = 3.0 ** position
    return base * col_scale[:, None] * (trend * row_scale)[None, :]


def draw_temporal(key, part):
    return covariance(jax.random.fold_in(key, 11), DAYS).astype(jnp.bfloat16)


def draw_spatial_lat(key, part):
    return covariance(jax.random.fold_in(key, 12), LAT).astype(jnp.bfloat16)


def draw_spatial_lon(key, part):
    return covariance(jax.random.fold_in(key, 13), LON).astype(jnp.bfloat16)


def draw_residual(key, part):
    return state_draw(key, 21)


def draw_direction(key, part):
    return state_draw(key, 22)


def touch_ends(drawn, key, low, largest):
    place = [jax.random.randint(jax.random.fold_in(key, axis), (), 0, length) for axis, length in enumerate(drawn.shape)]
    widest = drawn.shape.index(max(drawn.shape))
    neighbour = place[:widest] + [(place[widest] + 1) % drawn.shape[widest]] + place[widest + 1:]
    return drawn.at[tuple(place)].set(low).at[tuple(neighbour)].set(largest)


def level_of(stream_key, shape, pieces, least, top_value):
    def one(dim, blocks):
        heights = jax.random.uniform(jax.random.fold_in(jax.random.fold_in(stream_key, 6), dim), (blocks,), jnp.float32, least / len(pieces), top_value / len(pieces))
        return jnp.repeat(jnp.exp(heights), shape[dim] // blocks).reshape((-1,) + (1,) * (len(shape) - dim - 1))

    level = one(*pieces[0])
    for cut in pieces[1:]:
        level = level * one(*cut)
    return level


def routed_block(own_key, own, number, rows, count, top, reach, lean):
    sequence = jax.random.permutation(own_key, count)
    packed, usual = load_shares(count, rows * top, reach, lean, True), load_shares(count, rows * top, reach, lean, False)
    places = jnp.arange(count)

    def named(sizes, rotation):
        used = int((sizes > 0).sum())
        fixed = max(1, used // 4)
        moved = fixed + (places - fixed + rotation * (used - fixed)) % max(1, count - fixed)
        return jnp.zeros((count,), jnp.int32).at[sequence[jnp.where(places < fixed, places, moved)]].set(jnp.asarray(sizes, jnp.int32))

    sizes = jnp.where(number % 4 == 0, named(packed, number // 4), named(usual, number - number // 4 - 1))
    mixed = jax.random.permutation(jax.random.fold_in(own, 3), count)
    giver, sink = mixed[0:count // 2 * 2:2], mixed[1:count // 2 * 2:2]
    margin = jnp.minimum(sizes[giver] - 1, reach - sizes[sink]) // 2
    margin = jnp.where((giver == sequence[0]) | (sink == sequence[0]) | (sizes[sink] == 0), 0, jnp.maximum(margin, 0))
    moved = jax.random.randint(jax.random.fold_in(own, 4), (count // 2,), 0, 1 << 20) % (margin + 1)
    sizes = sizes.at[giver].add(-moved).at[sink].add(moved)
    members = jnp.searchsorted(jnp.cumsum(sizes), jnp.arange(rows * top), side="right").astype(jnp.int32)
    table = members.reshape(top, rows).T
    table = table[jax.random.permutation(jax.random.fold_in(own, 1), rows)]
    rotation = jax.random.randint(jax.random.fold_in(own, 2), (rows, 1), 0, top)
    return jnp.take_along_axis(table, (jnp.arange(top)[None, :] + rotation) % top, axis=1)


def load_shares(amount, total, bound, slope, full):
    portions = [(1 << 20) // math.isqrt(standing ** slope) + 1 for standing in range(1, amount + 1)]
    largest = bound if full else min(bound, max(-(-total // amount), total * portions[0] // sum(portions)))
    least = 1 if total - largest >= amount - 1 else 0
    counts, spare = [largest] + [least] * (amount - 1), total - largest - least * (amount - 1)
    while spare > 0:
        candidates = [i for i in range(1, amount) if counts[i] < largest] or [i for i in range(1, amount) if counts[i] < bound]
        pool, remaining = sum([portions[i] for i in candidates]), spare
        for i in candidates:
            addition = min(bound - counts[i], max(1, remaining * portions[i] // pool), spare)
            counts[i] = counts[i] + addition
            spare = spare - addition
    return np.array(counts)


def centred(rng, dims, deviation, reach, pieces=(), kind=jnp.bfloat16):
    array = jax.random.normal(rng, dims, jnp.float32) * deviation
    if len(pieces) > 0:
        array = level_of(rng, dims, pieces, -0.22, 0.18) * array
    return jnp.clip(array, min=-reach, max=reach).astype(kind)


def setup_inputs(seed: int = 0) -> dict:
    key_of = jax.random.split(jax.random.key(seed), 11)
    solution = centred(key_of[0], (RHS, OBS), 1.0, 6.0, ((1, 32),), jnp.float32)
    residual = draw_residual(jax.random.fold_in(key_of[10], 71), 0)
    direction = draw_direction(jax.random.fold_in(key_of[10], 71), 0)
    error_var = jnp.clip(jnp.exp(math.log(2.0) - 2.0794415 * jax.random.uniform(key_of[3], (OBS,), jnp.float32) ** level_of(key_of[3], (OBS,), ((0, 32),), -0.2, 0.2)), 0.25, 2.0)
    footprint = centred(key_of[4], (OBS, NT, LON), (NT * LON) ** -0.5, 0.25, ((0, 32),))
    tiles = touch_ends(jax.random.randint(key_of[5], (OBS, NT), 0, TILES), jax.random.fold_in(key_of[5], 1), 0, TILES - 1).astype(jnp.int32)
    window_keys = jax.random.split(jax.random.fold_in(key_of[6], 1), OBS // OBS_DEV)
    window_turns = jax.random.permutation(jax.random.fold_in(key_of[6], 3), OBS // OBS_DEV)
    window = jax.vmap(lambda own, number: routed_block(jax.random.fold_in(key_of[6], 2), own, number, OBS_DEV, N_WIDE, 1, CAP, 1))(window_keys, window_turns).reshape((OBS, 1))
    temporal = draw_temporal(jax.random.fold_in(key_of[10], 71), 0)
    spatial_lat = draw_spatial_lat(jax.random.fold_in(key_of[10], 71), 0)
    spatial_lon = draw_spatial_lon(jax.random.fold_in(key_of[10], 71), 0)
    return {"solution": solution, "residual": residual, "direction": direction, "error_var": error_var, "footprint": footprint, "tiles": tiles, "window": window, "temporal": temporal, "spatial_lat": spatial_lat, "spatial_lon": spatial_lon}


HIGHEST = lax.Precision.HIGHEST

def chol_solve(matrix, right):
    chol_low = jnp.linalg.cholesky(matrix)
    half_solve = lax.linalg.triangular_solve(chol_low, right, left_side=True, lower=True)
    return lax.linalg.triangular_solve(chol_low, half_solve, left_side=True, lower=True, transpose_a=True)

def gram_matrix(left, right):
    return jnp.dot(left, right.T, precision=HIGHEST)

def reference(solution, residual, direction, error_var, footprint, tiles, window, temporal, spatial_lat, spatial_lon):
    obs_total = footprint.shape[0]
    obs_index = jnp.arange(obs_total, dtype=jnp.int32)
    band_index = obs_index // OBS_DEV % N_NARROW
    day_index = window[:, 0][:, None] * DAY_DEV + tiles // LATB
    lat_index = band_index[:, None] * LATB + tiles % LATB
    cell_index = (day_index * LAT + lat_index).astype(jnp.int32)
    dir_half = direction.astype(jnp.bfloat16)
    block_rows = math.gcd(obs_total, 4096)
    block_count = obs_total // block_rows
    foot_blocks = footprint.reshape(block_count, block_rows, NT, LON)
    dir_blocks = dir_half.T.reshape(block_count, block_rows, RHS)
    cell_blocks = cell_index.reshape(block_count, block_rows * NT)

    def adjoint_step(accum, inputs):
        foot_block, dir_block, cell_block = inputs
        contrib = foot_block.astype(jnp.float32)[:, :, None, :] * dir_block.astype(jnp.float32)[:, None, :, None]
        return (accum.at[cell_block].add(contrib.reshape(block_rows * NT, RHS * LON)), None)
    start_accum = jnp.zeros((DAYS * LAT, RHS * LON), jnp.float32)
    accum, _ = lax.scan(adjoint_step, start_accum, (foot_blocks, dir_blocks, cell_blocks))
    fluxes = accum.astype(jnp.bfloat16).reshape(DAYS, LAT, RHS, LON)
    timed_flux = jnp.einsum('ts,sarl->tarl', temporal.astype(jnp.float32), fluxes.astype(jnp.float32)).astype(jnp.bfloat16)
    spread_lat = jnp.einsum('ab,tbrl->tarl', spatial_lat.astype(jnp.float32), timed_flux.astype(jnp.float32)).astype(jnp.bfloat16)
    smoothed = jnp.einsum('tarm,lm->tarl', spread_lat.astype(jnp.float32), spatial_lon.astype(jnp.float32)).astype(jnp.bfloat16)
    flux_table = smoothed.reshape(DAYS * LAT, RHS * LON)

    def forward_step(accum_dummy, inputs):
        foot_block, cell_block = inputs
        picked = flux_table[cell_block].reshape(block_rows, NT, RHS, LON).astype(jnp.float32)
        return (accum_dummy, jnp.einsum('bkrl,bkl->rb', picked, foot_block.astype(jnp.float32)))
    _, model_blocks = lax.scan(forward_step, jnp.zeros((), jnp.float32), (foot_blocks, cell_blocks))
    model_part = jnp.transpose(model_blocks, (1, 0, 2)).reshape(RHS, obs_total)
    model_image = model_part + error_var[None, :] * direction
    curvature = gram_matrix(direction, model_image)
    sym = 0.5 * (curvature + curvature.T)
    res_norm = gram_matrix(residual, residual)
    step_matrix = chol_solve(sym, res_norm)
    solution_new = solution + jnp.dot(step_matrix.T, direction, precision=HIGHEST)
    residual_new = residual - jnp.dot(step_matrix.T, model_image, precision=HIGHEST)
    norm_new = gram_matrix(residual_new, residual_new)
    ratio_matrix = chol_solve(res_norm, norm_new)
    direction_new = residual_new + jnp.dot(ratio_matrix.T, direction, precision=HIGHEST)
    return (solution_new, residual_new, direction_new)
```

```python
import functools

import jax
import jax.numpy as jnp
from jax import lax
from jax.experimental import pallas as pl
from jax.experimental.pallas import tpu as pltpu
from jax.sharding import PartitionSpec as P

HIGHEST = lax.Precision.HIGHEST
VMEM_LIMIT = 66 * 1000 * 1000
GROUP = 32


def chol_solve(matrix, right):
    chol_low = jnp.linalg.cholesky(matrix)
    half_solve = lax.linalg.triangular_solve(chol_low, right, left_side=True, lower=True)
    return lax.linalg.triangular_solve(
        chol_low, half_solve, left_side=True, lower=True, transpose_a=True
    )


def gram_matrix(left, right):
    return jnp.dot(left, right.T, precision=HIGHEST)


def adjoint_kernel(
    dims, cells, wins, me_ref, foot, dirs, equal, mix, out, picked, count, acc
):
    n_src, n_tiles, obs_dev, days, lat_band, rhs = dims
    lanes = foot.shape[-1]
    table_rows = acc.shape[0]
    chunk = 256

    @pl.loop(0, table_rows // chunk)
    def _(step):
        acc[pl.ds(pl.multiple_of(step * chunk, chunk), chunk), :] = jnp.zeros(
            (chunk, lanes), jnp.float32
        )

    me = me_ref[0]
    groups = obs_dev // GROUP

    def body(step, found):
        src = step // groups
        local = (step % groups) * GROUP
        base = src * obs_dev + local
        rows = [
            foot[
                pl.ds(pl.multiple_of((src * n_tiles + k) * obs_dev + local, GROUP), GROUP), :
            ].astype(jnp.float32)
            for k in range(n_tiles)
        ]
        same = equal[pl.ds(pl.multiple_of(base, GROUP), GROUP), :]
        sums = []
        pair = 0
        for k in range(n_tiles):
            total = rows[k]
            for m in range(k):
                total = total + same[:, pair : pair + 1] * rows[m]
                pair += 1
            sums.append(total)
        weights = dirs[step]
        for j in range(GROUP):
            weight = jnp.broadcast_to(weights[:, j : j + 1], (rhs, lanes))
            place = [
                pl.ds(pl.multiple_of(cells[(base + j) * n_tiles + k], rhs), rhs)
                for k in range(n_tiles)
            ]
            old = [acc[place[k], :] for k in range(n_tiles)]
            for k in range(n_tiles):
                acc[place[k], :] = old[k] + weight * sums[k][j : j + 1, :]
            picked[found] = base + j
            found = found + (wins[base + j] == me).astype(jnp.int32)
        return found

    count[0] = lax.fori_loop(0, n_src * groups, body, jnp.int32(0))

    @pl.loop(0, lat_band)
    def _(lat):
        for r in range(0, rhs, 2):
            both = jnp.concatenate(
                [
                    acc[pl.ds(lat * (days * rhs) + r + q, days, stride=rhs), :].astype(jnp.bfloat16)
                    for q in range(2)
                ],
                1,
            )
            mixed = jnp.dot(mix[...], both, preferred_element_type=jnp.float32)
            mixed = mixed.astype(out.dtype)
            out[lat * rhs + r] = mixed[:, :lanes]
            out[lat * rhs + r + 1] = mixed[:, lanes:]


def forward_kernel(dims, cells, picked, count, foot, spread, lon_t, out, wide_foot, table, parts):
    n_tiles, obs_dev, day_dev, rhs, group = dims
    lanes = foot.shape[-1]
    chunk = 256

    @pl.loop(0, foot.shape[0] // chunk)
    def _(step):
        block = pl.ds(pl.multiple_of(step * chunk, chunk), chunk)
        wide_foot[block, :] = foot[block, :].astype(jnp.float32)

    rows = table.shape[0]

    @pl.loop(0, rows // chunk)
    def _(step):
        block = pl.ds(pl.multiple_of(step * chunk, chunk), chunk)
        table[block, :] = (
            jnp.dot(spread[block, :], lon_t[...], preferred_element_type=jnp.float32)
            .astype(jnp.bfloat16)
            .astype(jnp.float32)
        )

    @pl.loop(0, out.shape[0] // chunk)
    def _(step):
        block = pl.ds(pl.multiple_of(step * chunk, chunk), chunk)
        out[block, :] = jnp.zeros((chunk, rhs), jnp.float32)

    total = count[0]

    @pl.loop(0, (total + group - 1) // group)
    def _(step):
        names = []
        for j in range(group):
            name = picked[jnp.minimum(step * group + j, total - 1)]
            names.append(name)
            first = name + (name // obs_dev) * ((n_tiles - 1) * obs_dev)
            value = None
            for k in range(n_tiles):
                cell = table[pl.ds(cells[name * n_tiles + k], rhs, stride=day_dev), :]
                row = wide_foot[pl.ds(first + k * obs_dev, 1), :]
                term = cell * row
                value = term if value is None else value + term
            parts[j] = value
        reduced = jnp.sum(parts[...], axis=-1)
        for j in range(group):
            out[pl.ds(names[j], 1), :] = reduced[j : j + 1, :]


def sum_kernel(n_wide, n_narrow, x_ref, out_ref, held, send_sem, recv_sem):
    count = n_wide * n_narrow
    me = lax.axis_index("wide") * n_narrow + lax.axis_index("narrow")
    barrier = pltpu.get_barrier_semaphore()

    def coords(who):
        return (who // n_narrow, who % n_narrow)

    @pl.loop(1, count)
    def _(step):
        pl.semaphore_signal(
            barrier,
            inc=1,
            device_id=coords((me + step) % count),
            device_id_type=pl.DeviceIdType.MESH,
        )

    pl.semaphore_wait(barrier, count - 1)

    def transfer(step):
        return pltpu.make_async_remote_copy(
            src_ref=x_ref,
            dst_ref=held.at[step],
            send_sem=send_sem.at[step],
            recv_sem=recv_sem.at[step],
            device_id=coords((me + step) % count),
            device_id_type=pl.DeviceIdType.MESH,
        )

    @pl.loop(1, count)
    def _(step):
        transfer(step).start()

    @pl.loop(1, count)
    def _(step):
        transfer(step).wait()

    held[0] = x_ref[...]

    def add(src, total):
        return total + held[(me - src + count) % count]

    out_ref[...] = lax.fori_loop(0, count, add, jnp.zeros(x_ref.shape, jnp.float32))


def sum_everywhere(x, n_wide, n_narrow, collective_id):
    count = n_wide * n_narrow
    rows, cols = x.shape
    padded = jnp.pad(x, ((0, 0), (0, 128 - cols)))
    return pl.pallas_call(
        functools.partial(sum_kernel, n_wide, n_narrow),
        out_shape=jax.ShapeDtypeStruct(padded.shape, jnp.float32),
        in_specs=[pl.BlockSpec(memory_space=pltpu.VMEM)],
        out_specs=pl.BlockSpec(memory_space=pltpu.VMEM),
        scratch_shapes=[
            pltpu.VMEM((count,) + padded.shape, jnp.float32),
            pltpu.SemaphoreType.DMA((count,)),
            pltpu.SemaphoreType.DMA((count,)),
        ],
        compiler_params=pltpu.CompilerParams(collective_id=collective_id, has_side_effects=True),
    )(padded)[:, :cols]


def on_device(
    solution,
    residual,
    direction,
    error_var,
    footprint,
    tiles,
    window,
    temporal,
    spatial_lat,
    spatial_lon,
):
    n_wide = lax.axis_size("wide")
    n_narrow = lax.axis_size("narrow")
    rhs, obs_dev = direction.shape
    days = temporal.shape[0]
    day_dev = days // n_wide
    lat_total = spatial_lat.shape[0]
    lat_band = lat_total // n_narrow
    lanes = spatial_lon.shape[0]
    n_tiles = tiles.shape[1]
    obs = n_wide * obs_dev
    wide_index = lax.axis_index("wide")
    narrow_index = lax.axis_index("narrow")
    smem = pl.BlockSpec(memory_space=pltpu.SMEM)
    vmem = pl.BlockSpec(memory_space=pltpu.VMEM)

    day_local, lat_local = tiles // lat_band, tiles % lat_band
    adjoint_cells = (lat_local * days + window * day_dev + day_local) * rhs
    forward_cells = lat_local * (rhs * day_dev) + day_local
    pairs = [(m, k) for k in range(n_tiles) for m in range(k)]
    equal = jnp.stack([(tiles[:, m] == tiles[:, k]) for m, k in pairs], 1).astype(jnp.int32)
    meta = jnp.concatenate(
        [adjoint_cells.reshape(-1), forward_cells.reshape(-1), window.reshape(-1), equal.reshape(-1)]
    )
    dir_half = direction.astype(jnp.bfloat16)
    floats = jnp.concatenate(
        [
            footprint.transpose(1, 0, 2).reshape(n_tiles * obs_dev, lanes),
            dir_half.reshape(rhs * obs_dev // lanes, lanes),
        ],
        0,
    )
    all_floats = lax.all_gather(floats, "wide", axis=0)
    all_meta = lax.all_gather(meta, "wide", axis=0)
    foot = all_floats[:, : n_tiles * obs_dev].reshape(n_wide * n_tiles * obs_dev, lanes)
    dirs = (
        all_floats[:, n_tiles * obs_dev :]
        .reshape(n_wide, rhs, obs_dev // GROUP, GROUP)
        .transpose(0, 2, 1, 3)
        .reshape(obs // GROUP, rhs, GROUP)
        .astype(jnp.float32)
    )
    cut = n_tiles * obs_dev
    cells_adj = all_meta[:, :cut].reshape(-1)
    cells_fwd = all_meta[:, cut : 2 * cut].reshape(-1)
    wins = all_meta[:, 2 * cut : 2 * cut + obs_dev].reshape(-1)
    same = all_meta[:, 2 * cut + obs_dev :].reshape(obs, len(pairs)).astype(jnp.float32)
    mix = lax.dynamic_slice_in_dim(temporal, wide_index * day_dev, day_dev, 0)

    timed, picked, count = pl.pallas_call(
        functools.partial(
            adjoint_kernel, (n_wide, n_tiles, obs_dev, days, lat_band, rhs)
        ),
        out_shape=(
            jax.ShapeDtypeStruct((lat_band * rhs, day_dev, lanes), jnp.bfloat16),
            jax.ShapeDtypeStruct((obs,), jnp.int32),
            jax.ShapeDtypeStruct((1,), jnp.int32),
        ),
        in_specs=[smem, smem, smem, vmem, vmem, vmem, vmem],
        out_specs=(vmem, smem, smem),
        scratch_shapes=[pltpu.VMEM((lat_band * days * rhs, lanes), jnp.float32)],
        compiler_params=pltpu.CompilerParams(vmem_limit_bytes=VMEM_LIMIT),
    )(cells_adj, wins, wide_index.reshape(1).astype(jnp.int32), foot, dirs, same, mix)

    gathered = lax.all_gather(
        timed.reshape(lat_band, rhs * day_dev * lanes), "narrow", axis=0, tiled=True
    )
    lat_rows = lax.dynamic_slice_in_dim(spatial_lat, narrow_index * lat_band, lat_band, 0)
    spread = jnp.dot(lat_rows, gathered, preferred_element_type=jnp.float32).astype(jnp.bfloat16)
    spread = spread.reshape(lat_band * rhs * day_dev, lanes)

    group = 16
    model = pl.pallas_call(
        functools.partial(forward_kernel, (n_tiles, obs_dev, day_dev, rhs, group)),
        out_shape=jax.ShapeDtypeStruct((obs, rhs), jnp.float32),
        in_specs=[smem, smem, smem, vmem, vmem, vmem],
        out_specs=vmem,
        scratch_shapes=[
            pltpu.VMEM((n_wide * n_tiles * obs_dev, lanes), jnp.float32),
            pltpu.VMEM((lat_band * rhs * day_dev, lanes), jnp.float32),
            pltpu.VMEM((group, rhs, lanes), jnp.float32),
        ],
        compiler_params=pltpu.CompilerParams(vmem_limit_bytes=VMEM_LIMIT),
    )(cells_fwd, picked, count, foot, spread, spatial_lon.T)

    home = lax.all_to_all(
        model.reshape(n_wide, obs_dev * rhs), "wide", split_axis=0, concat_axis=0, tiled=True
    )
    model_part = home.sum(axis=0).reshape(obs_dev, rhs).T
    model_image = model_part + error_var[None, :] * direction
    sums = sum_everywhere(
        jnp.concatenate(
            [gram_matrix(direction, model_image), gram_matrix(residual, residual)], 1
        ),
        n_wide,
        n_narrow,
        1,
    )
    curvature, res_norm = sums[:, :rhs], sums[:, rhs:]
    sym = 0.5 * (curvature + curvature.T)
    step_matrix = chol_solve(sym, res_norm)
    residual_new = residual - jnp.dot(step_matrix.T, model_image, precision=HIGHEST)
    norm_new = sum_everywhere(gram_matrix(residual_new, residual_new), n_wide, n_narrow, 2)
    solution_new = solution + jnp.dot(step_matrix.T, direction, precision=HIGHEST)
    ratio_matrix = chol_solve(res_norm, norm_new)
    direction_new = residual_new + jnp.dot(ratio_matrix.T, direction, precision=HIGHEST)
    return (solution_new, residual_new, direction_new)


def solution(mesh):
    split = ("wide", "narrow")
    in_specs = (
        P(None, split),
        P(None, split),
        P(None, split),
        P(split),
        P(split, None, None),
        P(split, None),
        P(split, None),
        P(),
        P(),
        P(),
    )
    out_specs = (P(None, split), P(None, split), P(None, split))
    return jax.shard_map(
        on_device, mesh=mesh, in_specs=in_specs, out_specs=out_specs, check_vma=False
    )
```
